32 devices in a mesh: row: 4 (over y, x), col: 8 (over z, core).
Axes of the slice: x: 2, y: 2, z: 4, core: 2. Of those that a mesh axis runs over, the one named last changes fastest.
Arguments:
- cam_jac: bfloat16 [2, 2, 6, 512, 1024], P(None, None, None, ('row', 'col')), may hold values from -0.09375 to 0.09375
- pt_jac: bfloat16 [2, 2, 3, 512, 1024], P(None, None, None, ('row', 'col')), may hold values from -6 to 6
- resid: bfloat16 [2, 2, 512, 1024], P(None, None, ('row', 'col')), may hold values from -6 to 6
- partner: int32 [512, 1024], P(('row', 'col')), may hold values from 0 to 511, as said below
- count: int32 [512], P(('row', 'col')), may hold values from 512 to 1024
- tile_map: int32 [512], replicated, may hold values from 0 to 511, as said below
Outputs:
- coupling: bfloat16 [6, 6, 512, 512], P(None, None, 'row', 'col')
- camera_update: float32 [6, 512], P(None, 'row')
- residual: float32 [6, 512], P(None, 'row')
The draws below stay inside these ranges and needn't reach their ends.
Inputs may be any that keep to these rules, and one draw needn't show every extreme that they name: partner[a, t] is never a. `tile_map`: a permutation of the tile positions; of the 16 consecutive scenes of each device, exactly 4 have positions in each block of 128 consecutive positions.
All inputs are finite; a program needn't handle non-finite values.
Results may differ from the reference program's by a relative error of at most 0.0015.
Values may be sent and summed in bfloat16 or wider, within the bound.
A program may use at most 64 MiB of HBM per device.

```python
import jax
import jax.numpy as jnp
from jax import lax

SCN_DEV = 16
PTS = 1024
ITERS = 3
SCENES = 512
TILE_ROWS = 128
PER_GROUP = 4


def draw_partner(key, part):
    scene_ids = jnp.arange(SCENES, dtype=jnp.int32)[:, None]
    offsets = jax.random.randint(key, (SCENES, PTS), 1, SCENES, dtype=jnp.int32)
    return ((scene_ids + offsets) % SCENES).astype(jnp.int32)


def draw_tile_map(key, part):
    devices = SCENES // SCN_DEV
    groups = SCENES // TILE_ROWS
    first_key, second_key = jax.random.split(jax.random.fold_in(key, 7))
    scores = jax.random.randint(first_key, (devices, SCN_DEV), 0, 1 << 14, dtype=jnp.int32) * SCN_DEV
    scores = scores + jnp.arange(SCN_DEV, dtype=jnp.int32)[None, :]
    local_rank = jnp.argsort(jnp.argsort(scores, axis=1), axis=1).astype(jnp.int32)
    group_of = local_rank // PER_GROUP
    within = jnp.arange(devices, dtype=jnp.int32)[:, None] * PER_GROUP + local_rank % PER_GROUP
    scores_two = jax.random.randint(second_key, (groups, TILE_ROWS), 0, 1 << 14, dtype=jnp.int32) * TILE_ROWS
    scores_two = scores_two + jnp.arange(TILE_ROWS, dtype=jnp.int32)[None, :]
    shuffle = jnp.argsort(jnp.argsort(scores_two, axis=1), axis=1).astype(jnp.int32)
    tiles = group_of * TILE_ROWS + shuffle[group_of, within]
    return tiles.reshape(SCENES).astype(jnp.int32)


def place_ends(values, own_key, least, top_value):
    longest = values.shape.index(max(values.shape))
    spots = []
    for shift in (0, 1):
        where = [jax.random.randint(jax.random.fold_in(own_key, axis), (), 0, length) for axis, length in enumerate(values.shape)]
        where[longest] = (where[longest] + shift) % values.shape[longest]
        spots.append(tuple(where))
    return values.at[spots[0]].set(least).at[spots[1]].set(top_value)


def steps_of(key, extent, pieces, least, top_value):
    factor_of, own = 1.0, jax.random.fold_in(key, 6)
    for position, parts in pieces:
        heights = jnp.exp(jax.random.uniform(jax.random.fold_in(own, position), (parts,), jnp.float32, least / len(pieces), top_value / len(pieces)))
        factor_of = factor_of * jnp.repeat(heights, extent[position] // parts).reshape([-1 if axis == position else 1 for axis in range(len(extent))])
    return factor_of


def bell_draw(key, shape, scale, most, pieces=(), held_as=jnp.bfloat16):
    entries = scale * jax.random.normal(key, shape, jnp.float32)
    if pieces:
        entries = entries * steps_of(key, shape, pieces, -0.22, 0.18)
    return jnp.clip(entries, -most, most).astype(held_as)


def setup_inputs(seed: int = 0) -> dict:
    key_of = jax.random.split(jax.random.key(seed), 7)
    cam_jac = bell_draw(key_of[0], (2, 2, 6, SCENES, PTS), (4 * PTS) ** -0.5, 0.09375, ((3, 32),))
    pt_jac = bell_draw(key_of[1], (2, 2, 3, SCENES, PTS), 1.0, 6.0, ((3, 32),))
    resid = bell_draw(key_of[2], (2, 2, SCENES, PTS), 1.0, 6.0, ((2, 32),))
    partner = draw_partner(jax.random.fold_in(key_of[6], 71), 0)
    count = place_ends(jax.random.randint(key_of[4], (SCENES,), PTS // 2, PTS + 1), jax.random.fold_in(key_of[4], 1), PTS // 2, PTS).astype(jnp.int32)
    tile_map = draw_tile_map(jax.random.fold_in(key_of[6], 71), 0)
    return dict(cam_jac=cam_jac, pt_jac=pt_jac, resid=resid, partner=partner, count=count, tile_map=tile_map)


CAMERA_DAMPING = 1.0
POINT_DAMPING = 1.0


def cross_product(first_vec, second_vec):
    return jnp.stack([first_vec[1] * second_vec[2] - first_vec[2] * second_vec[1],
                      first_vec[2] * second_vec[0] - first_vec[0] * second_vec[2],
                      first_vec[0] * second_vec[1] - first_vec[1] * second_vec[0]], axis=0)


def point_terms(camera, points_jac, errors):
    camera = camera.astype(jnp.float32)
    points_jac = points_jac.astype(jnp.float32)
    errors = errors.astype(jnp.float32)
    own_jac, other_jac = camera[0], camera[1]
    own_point, other_point = points_jac[0], points_jac[1]
    own_error, other_error = errors[0], errors[1]
    point_hessian = jnp.sum(own_point[:, :, None] * own_point[:, None, :], axis=0)
    point_hessian = point_hessian + jnp.sum(other_point[:, :, None] * other_point[:, None, :], axis=0)
    point_hessian = point_hessian + POINT_DAMPING * jnp.eye(3, dtype=jnp.float32)[:, :, None, None]
    first_row, second_row, third_row = point_hessian[0], point_hessian[1], point_hessian[2]
    cofactor_first = cross_product(second_row, third_row)
    cofactor_second = cross_product(third_row, first_row)
    cofactor_third = cross_product(first_row, second_row)
    determinant = jnp.sum(first_row * cofactor_first, axis=0)
    inverse = jnp.stack([cofactor_first, cofactor_second, cofactor_third], axis=1) / determinant
    w_own = jnp.sum(own_jac[:, :, None] * own_point[:, None, :], axis=0)
    w_other = jnp.sum(other_jac[:, :, None] * other_point[:, None, :], axis=0)
    point_rhs = -(jnp.sum(own_point * own_error[:, None], axis=0) + jnp.sum(other_point * other_error[:, None], axis=0))
    own_vi = jnp.sum(w_own[:, :, None] * inverse[None, :, :], axis=1)
    other_vi = jnp.sum(w_other[:, :, None] * inverse[None, :, :], axis=1)
    diag_own = jnp.sum(own_jac[:, :, None] * own_jac[:, None, :], axis=0) - jnp.sum(own_vi[:, None, :] * w_own[None, :, :], axis=2)
    diag_other = jnp.sum(other_jac[:, :, None] * other_jac[:, None, :], axis=0) - jnp.sum(other_vi[:, None, :] * w_other[None, :, :], axis=2)
    link = -jnp.sum(own_vi[:, None, :] * w_other[None, :, :], axis=2)
    grad_own = -jnp.sum(own_jac * own_error[:, None], axis=0) - jnp.sum(own_vi * point_rhs[None], axis=1)
    grad_other = -jnp.sum(other_jac * other_error[:, None], axis=0) - jnp.sum(other_vi * point_rhs[None], axis=1)
    return diag_own, diag_other, link, grad_own, grad_other


def reference(cam_jac, pt_jac, resid, partner, count, tile_map):
    blocks = SCENES // SCN_DEV

    def split_scenes(array):
        lead = array.shape[:-2]
        shaped = array.reshape(lead + (blocks, SCN_DEV, PTS))
        return jnp.moveaxis(shaped, len(lead), 0)

    inputs = (split_scenes(cam_jac), split_scenes(pt_jac), split_scenes(resid),
              partner.reshape(blocks, SCN_DEV, PTS), count.reshape(blocks, SCN_DEV),
              tile_map.reshape(blocks, SCN_DEV))

    def add_block(sums_so_far, block):
        coupling_flat, diag_sum, grad_sum = sums_so_far
        camera, points_jac, errors, partner_block, count_block, tile_block = block
        diag_own, diag_other, link, grad_own, grad_other = point_terms(camera, points_jac, errors)
        active = (jnp.arange(PTS, dtype=jnp.int32)[None, :] < count_block[:, None]).astype(jnp.float32)
        tile_other = jnp.take(tile_map, partner_block).astype(jnp.int32).reshape(-1)
        tile_own = jnp.broadcast_to(tile_block[:, None], (SCN_DEV, PTS)).astype(jnp.int32).reshape(-1)
        target = tile_own * SCENES + tile_other
        coupling_flat = coupling_flat.at[:, target].add((link * active).reshape(36, -1))
        diag_sum = diag_sum.at[:, tile_own].add((diag_own * active).reshape(36, -1))
        diag_sum = diag_sum.at[:, tile_other].add((diag_other * active).reshape(36, -1))
        grad_sum = grad_sum.at[:, tile_own].add((grad_own * active).reshape(6, -1))
        grad_sum = grad_sum.at[:, tile_other].add((grad_other * active).reshape(6, -1))
        return (coupling_flat, diag_sum, grad_sum), None

    start = (jnp.zeros((36, SCENES * SCENES), jnp.float32), jnp.zeros((36, SCENES), jnp.float32),
             jnp.zeros((6, SCENES), jnp.float32))
    (coupling_flat, diag_sum, grad_sum), unused = lax.scan(add_block, start, inputs)
    coupling = coupling_flat.reshape(6, 6, SCENES, SCENES).astype(jnp.bfloat16)
    coupling_wide = coupling.astype(jnp.float32)
    diag_blocks = diag_sum.reshape(6, 6, SCENES)

    def operator(vector):
        result = CAMERA_DAMPING * vector
        result = result + jnp.einsum('xyi,yi->xi', diag_blocks, vector, precision=lax.Precision.HIGHEST)
        result = result + jnp.einsum('xyij,yj->xi', coupling_wide, vector, precision=lax.Precision.HIGHEST)
        result = result + jnp.einsum('xyij,xi->yj', coupling_wide, vector, precision=lax.Precision.HIGHEST)
        return result

    solution = jnp.zeros((6, SCENES), jnp.float32)
    remainder = grad_sum
    direction = grad_sum
    norm_now = jnp.sum(remainder * remainder)
    for iteration in range(ITERS):
        product_vec = operator(direction)
        step_size = norm_now / jnp.sum(direction * product_vec)
        solution = solution + step_size * direction
        remainder = remainder - step_size * product_vec
        norm_next = jnp.sum(remainder * remainder)
        direction = remainder + (norm_next / norm_now) * direction
        norm_now = norm_next
    return coupling, solution, remainder
```

```python
import functools

import jax
import jax.numpy as jnp
from jax import lax
from jax.experimental import pallas as pl
from jax.experimental.pallas import tpu as pltpu
from jax.sharding import PartitionSpec as P

ITERS = 3
CAMERA_DAMPING = 1.0
POINT_DAMPING = 1.0
LANES = 128
OTHER_ROWS = 64
OWN_ROWS = 32
ROWS = OTHER_ROWS + OWN_ROWS
PAIRS = [(x, y) for x in range(6) for y in range(x, 6)]
SPARE = [y * 8 + 6 + h for y in range(6) for h in range(2)] + list(range(48, 63))
NT = (((1,), (1,)), ((), ()))
MESH = pl.DeviceIdType.MESH
VMEM_LIMIT = 60 * 1024 * 1024


def total_of(terms):
    result = terms[0]
    for term in terms[1:]:
        result = result + term
    return result


def point_rows(cam, pt, err):
    hess = {}
    for i in range(3):
        for j in range(i, 3):
            value = total_of([pt[s][r][i] * pt[s][r][j] for s in range(2) for r in range(2)])
            hess[i, j] = value + POINT_DAMPING if i == j else value
    a, b, c = hess[0, 0], hess[0, 1], hess[0, 2]
    d, e, f = hess[1, 1], hess[1, 2], hess[2, 2]
    cof = {
        (0, 0): d * f - e * e,
        (0, 1): e * c - b * f,
        (0, 2): b * e - d * c,
        (1, 1): f * a - c * c,
        (1, 2): c * b - a * e,
        (2, 2): a * d - b * b,
    }
    scale = 1.0 / (a * cof[0, 0] + b * cof[0, 1] + c * cof[0, 2])
    inv = {key: value * scale for key, value in cof.items()}
    rhs = [-total_of([pt[s][r][i] * err[s][r] for s in range(2) for r in range(2)]) for i in range(3)]
    w = [
        [[total_of([cam[s][r][x] * pt[s][r][i] for r in range(2)]) for i in range(3)] for x in range(6)]
        for s in range(2)
    ]
    wv = [
        [
            [total_of([w[s][x][i] * inv[min(i, j), max(i, j)] for i in range(3)]) for j in range(3)]
            for x in range(6)
        ]
        for s in range(2)
    ]
    link = {
        (x, y): -total_of([wv[0][x][j] * w[1][y][j] for j in range(3)])
        for x in range(6)
        for y in range(6)
    }
    sides = []
    for s in range(2):
        rows = [
            total_of([cam[s][r][x] * cam[s][r][y] for r in range(2)])
            - total_of([wv[s][x][j] * w[s][y][j] for j in range(3)])
            for x, y in PAIRS
        ]
        rows += [
            -total_of([cam[s][r][x] * err[s][r] for r in range(2)])
            - total_of([wv[s][x][j] * rhs[j] for j in range(3)])
            for x in range(6)
        ]
        sides.append(rows)
    return link, sides[0], sides[1]


def assemble_kernel(
    nrow, ncol, cam_ref, pt_ref, err_ref, partner_ref, count_ref, map_ref, target_ref,
    mat_ref, diag_ref, grad_ref, panel_ref, vals, live_partner, acc,
):
    scn, points = partner_ref.shape
    scenes = map_ref.shape[1]
    blocks = points // LANES
    base = (lax.axis_index("row") * ncol + lax.axis_index("col")) * scn

    def point_block(jb, carry):
        lanes = pl.ds(pl.multiple_of(jb * LANES, LANES), LANES)
        take = lambda ref, *at: ref[at + (slice(None), lanes)].astype(jnp.float32)
        cam = [[[take(cam_ref, s, r, x) for x in range(6)] for r in range(2)] for s in range(2)]
        pt = [[[take(pt_ref, s, r, x) for x in range(3)] for r in range(2)] for s in range(2)]
        err = [[take(err_ref, s, r) for r in range(2)] for s in range(2)]
        slot = lax.broadcasted_iota(jnp.int32, (scn, LANES), 1) + jb * LANES
        active = slot < count_ref[...]
        live_partner[:, lanes] = jnp.where(active, partner_ref[:, lanes], -1)
        link, own, other = point_rows(cam, pt, err)

        def put(row, value):
            vals[pl.ds(jb * (scn * ROWS) + row, scn, stride=ROWS), :] = value

        zero = jnp.zeros((scn, LANES), jnp.float32)
        for (x, y), value in link.items():
            put(y * 8 + x, value)
        for u in range(27):
            put(SPARE[u], other[u])
            put(OTHER_ROWS + u, jnp.where(active, own[u], 0.0))
        put(OTHER_ROWS - 1, zero)
        for u in range(27, OWN_ROWS):
            put(OTHER_ROWS + u, zero)
        return carry

    lax.fori_loop(0, blocks, point_block, 0)
    acc[...] = jnp.zeros_like(acc)
    chunk = 256
    low = lax.broadcasted_iota(jnp.int32, (8, chunk), 0) < 6

    def scene(s, own_sum):
        start = lambda jb: pl.multiple_of((jb * scn + s) * ROWS, 8)
        full = jnp.concatenate([vals[pl.ds(start(jb), OTHER_ROWS), :] for jb in range(blocks)], axis=1)
        high = full.astype(jnp.bfloat16)
        rest = (full - high.astype(jnp.float32)).astype(jnp.bfloat16)
        both = jnp.concatenate([high, rest], axis=0)
        ids = live_partner[pl.ds(s, 1), :]
        for b in range(scenes // chunk):
            spot = lax.broadcasted_iota(jnp.int32, (chunk, points), 0) + b * chunk
            onehot = jnp.where(spot == ids, 1.0, 0.0).astype(jnp.bfloat16)
            sums = lax.dot_general(both, onehot, NT, preferred_element_type=jnp.float32)
            sums = sums[:OTHER_ROWS] + sums[OTHER_ROWS:]
            cols = slice(b * chunk, (b + 1) * chunk)
            acc[:, cols] += sums
            for y in range(6):
                part = jnp.where(low, sums[y * 8 : y * 8 + 8], 0.0)
                mat_ref[pl.ds(pl.multiple_of(s * 8, 8), 8), y * scenes + b * chunk : y * scenes + (b + 1) * chunk] = (
                    part.astype(jnp.bfloat16).astype(jnp.float32)
                )
        own = total_of([vals[pl.ds(start(jb) + OTHER_ROWS, OWN_ROWS), :] for jb in range(blocks)])
        own = jnp.sum(own, axis=1, keepdims=True)
        here = lax.broadcasted_iota(jnp.int32, (OWN_ROWS, scenes), 1) == base + s
        return own_sum + jnp.where(here, own, 0.0)

    own_sum = lax.fori_loop(0, scn, scene, jnp.zeros((OWN_ROWS, scenes), jnp.float32))
    diag_ref[...] = jnp.zeros_like(diag_ref)
    grad_ref[...] = jnp.zeros_like(grad_ref)
    for u in range(27):
        row = acc[SPARE[u] : SPARE[u] + 1, :] + own_sum[u : u + 1, :]
        if u < 21:
            x, y = PAIRS[u]
            diag_ref[y * 8 + x : y * 8 + x + 1, :] = row
            if x != y:
                diag_ref[x * 8 + y : x * 8 + y + 1, :] = row
        else:
            grad_ref[u - 21 : u - 20, :] = row

    rows = panel_ref.shape[1]
    order = jnp.where(
        lax.broadcasted_iota(jnp.int32, (nrow * rows, scn * 8), 0) == target_ref[...], 1.0, 0.0
    ).astype(jnp.bfloat16)
    spots = jnp.where(
        lax.broadcasted_iota(jnp.int32, (scenes, scenes), 0) == map_ref[...], 1.0, 0.0
    ).astype(jnp.bfloat16)
    width = scenes // ncol
    ordered = []
    for y in range(6):
        piece = mat_ref[:, y * scenes : (y + 1) * scenes].astype(jnp.bfloat16)
        piece = jnp.dot(order, piece, preferred_element_type=jnp.float32).astype(jnp.bfloat16)
        ordered.append(lax.dot_general(piece, spots, NT, preferred_element_type=jnp.float32))
    for c in range(ncol):
        wide = jnp.concatenate([o[:, c * width : (c + 1) * width] for o in ordered], axis=1)
        for r in range(nrow):
            panel_ref[r * ncol + c] = wide[r * rows : (r + 1) * rows].astype(jnp.bfloat16)


def iterate_kernel(
    nrow, ncol, scn, mat_ref, diag_ref, grad_ref, panel_ref, recv_ref, sol_ref, res_ref,
    buf_col, buf_row, send_p, recv_p, send_c, recv_c, send_r, recv_r,
):
    row, col = lax.axis_index("row"), lax.axis_index("col")
    count = nrow * ncol
    me = row * ncol + col
    base = me * scn
    scenes = grad_ref.shape[1]

    barrier = pltpu.get_barrier_semaphore()

    def greet(off, carry):
        peer = lax.rem(me + off, count)
        pl.semaphore_signal(barrier, inc=1, device_id=(peer // ncol, lax.rem(peer, ncol)), device_id_type=MESH)
        return carry

    lax.fori_loop(1, count, greet, 0)
    pl.semaphore_wait(barrier, count - 1)

    def panel_copy(off):
        peer = lax.rem(me + off, count)
        return pltpu.make_async_remote_copy(
            src_ref=panel_ref.at[peer],
            dst_ref=recv_ref.at[me],
            send_sem=send_p.at[off],
            recv_sem=recv_p.at[off],
            device_id=(peer // ncol, lax.rem(peer, ncol)),
            device_id_type=MESH,
        )

    def gathered(value, buf, spot, turn, size, send, recv, device_of, between=None):
        buf[turn, spot] = value
        copies = []
        for off in range(1, size):
            copy = pltpu.make_async_remote_copy(
                src_ref=buf.at[turn, spot],
                dst_ref=buf.at[turn, spot],
                send_sem=send.at[turn, off],
                recv_sem=recv.at[turn, off],
                device_id=device_of(lax.rem(spot + off, size)),
                device_id_type=MESH,
            )
            copy.start()
            copies.append(copy)
        if between is not None:
            between()
        for copy in copies:
            copy.wait()
        return total_of([buf[turn, i] for i in range(size)])

    def all_sum(value, turn, between=None):
        value = gathered(value, buf_col, col, turn, ncol, send_c, recv_c, lambda p: (row, p), between)
        return gathered(value, buf_row, row, turn, nrow, send_r, recv_r, lambda p: (p, col))

    def start_panels():
        def step(off, carry):
            panel_copy(off).start()
            return carry

        lax.fori_loop(1, count, step, 0)
        recv_ref[me] = panel_ref[me]

    lane = lax.broadcasted_iota(jnp.int32, (8, scenes), 1)

    def local_product(vector):
        flat = jnp.concatenate([vector[y : y + 1] for y in range(6)], axis=1)

        def step(s, carry):
            back, out = carry
            here = lane == base + s
            own = jnp.sum(jnp.where(here, vector, 0.0), axis=1, keepdims=True)
            part = mat_ref[pl.ds(pl.multiple_of(s * 8, 8), 8), :]
            ahead = jnp.sum(part * flat, axis=1, keepdims=True)
            return back + part * own, out + jnp.where(here, ahead, 0.0)

        zero = jnp.zeros((8, scenes), jnp.float32)
        back, out = lax.fori_loop(0, scn, step, (jnp.zeros((8, 6 * scenes), jnp.float32), zero))
        back = jnp.sum(back, axis=0, keepdims=True)
        for y in range(6):
            out = out + diag_ref[y * 8 : y * 8 + 8, :] * vector[y : y + 1]
        back = jnp.concatenate(
            [back[:, y * scenes : (y + 1) * scenes] for y in range(6)]
            + [jnp.zeros((2, scenes), jnp.float32)],
            axis=0,
        )
        return out + back

    def inner(first, second):
        return jnp.sum(jnp.sum(first * second, axis=1, keepdims=True), axis=0, keepdims=True)

    remainder = all_sum(grad_ref[...], 0, start_panels)
    result = jnp.zeros_like(remainder)
    direction = remainder
    norm_now = inner(remainder, remainder)
    for turn in range(ITERS):
        image = CAMERA_DAMPING * direction + all_sum(local_product(direction), turn + 1)
        size = norm_now / inner(direction, image)
        result = result + size * direction
        remainder = remainder - size * image
        norm_next = inner(remainder, remainder)
        direction = remainder + norm_next / norm_now * direction
        norm_now = norm_next
    sol_ref[...] = result
    res_ref[...] = remainder

    def finish(off, carry):
        panel_copy(off).wait()
        return carry

    lax.fori_loop(1, count, finish, 0)


def place_kernel(recv_ref, place_ref, map_ref, sol_ref, res_ref, coupling_ref, update_ref, residual_ref):
    tile_rows, width = coupling_ref.shape[2:]
    held = recv_ref.shape[0]
    for x in range(6):
        spot = lax.broadcasted_iota(jnp.int32, (tile_rows, held), 0) + x * tile_rows
        chosen = jnp.where(spot == place_ref[...], 1.0, 0.0).astype(jnp.bfloat16)
        block = jnp.dot(chosen, recv_ref[...], preferred_element_type=jnp.float32).astype(jnp.bfloat16)
        for y in range(6):
            coupling_ref[x, y] = block[:, y * width : (y + 1) * width]
    scenes = map_ref.shape[1]
    spot = lax.broadcasted_iota(jnp.int32, (tile_rows, scenes), 0) + lax.axis_index("row") * tile_rows
    chosen = jnp.where(spot == map_ref[...], 1.0, 0.0).astype(jnp.bfloat16)
    for source, target in ((sol_ref, update_ref), (res_ref, residual_ref)):
        left = source[...]
        moved = None
        for unused in range(3):
            short = left.astype(jnp.bfloat16)
            left = left - short.astype(jnp.float32)
            part = lax.dot_general(short, chosen, NT, preferred_element_type=jnp.float32)
            moved = part if moved is None else moved + part
        target[...] = moved[:6]


def shards(cam_jac, pt_jac, resid, partner, count, tile_map):
    nrow = lax.axis_size("row")
    ncol = lax.axis_size("col")
    scenes = tile_map.shape[0]
    scn, points = partner.shape
    devices = nrow * ncol
    tile_rows = scenes // nrow
    width = scenes // ncol
    group = scn // nrow
    rows = -(-6 * group // 8) * 8
    row_index = lax.axis_index("row")
    device = row_index * ncol + lax.axis_index("col")
    tiles = tile_map.reshape(devices, scn)
    rank = jnp.sum((tiles[:, None, :] < tiles[:, :, None]).astype(jnp.int32), axis=2)
    param = jnp.arange(8, dtype=jnp.int32)[None, :]
    rank_own = lax.dynamic_slice_in_dim(rank, device, 1, 0).reshape(scn, 1)
    target = (rank_own // group) * rows + param * group + rank_own % group
    target = jnp.where(param < 6, target, -1).reshape(1, scn * 8)
    wanted = jnp.arange(group, dtype=jnp.int32) + row_index * group
    held = jnp.sum(jnp.where(rank[:, None, :] == wanted[None, :, None], tiles[:, None, :], 0), axis=2)
    held = held - row_index * tile_rows
    place = held[:, None, :] + (jnp.arange(6, dtype=jnp.int32) * tile_rows)[None, :, None]
    place = place.reshape(devices, 6 * group)
    place = jnp.pad(place, ((0, 0), (0, rows - 6 * group)), constant_values=-1).reshape(1, devices * rows)
    map_row = tile_map.reshape(1, scenes)

    vmem = pl.BlockSpec(memory_space=pltpu.VMEM)
    f32 = jnp.float32
    mat, diag, grad, panel = pl.pallas_call(
        functools.partial(assemble_kernel, nrow, ncol),
        out_shape=(
            jax.ShapeDtypeStruct((scn * 8, 6 * scenes), f32),
            jax.ShapeDtypeStruct((48, scenes), f32),
            jax.ShapeDtypeStruct((8, scenes), f32),
            jax.ShapeDtypeStruct((devices, rows, 6 * width), jnp.bfloat16),
        ),
        in_specs=[vmem] * 7,
        out_specs=(vmem,) * 4,
        scratch_shapes=[
            pltpu.VMEM((points // LANES * scn * ROWS, LANES), f32),
            pltpu.VMEM((scn, points), jnp.int32),
            pltpu.VMEM((OTHER_ROWS, scenes), f32),
        ],
        compiler_params=pltpu.CompilerParams(vmem_limit_bytes=VMEM_LIMIT),
        name="assemble",
    )(cam_jac, pt_jac, resid, partner, count.reshape(scn, 1), map_row, target)

    turns = ITERS + 1
    dma = pltpu.SemaphoreType.DMA
    recv, sol, res = pl.pallas_call(
        functools.partial(iterate_kernel, nrow, ncol, scn),
        out_shape=(
            jax.ShapeDtypeStruct((devices, rows, 6 * width), jnp.bfloat16),
            jax.ShapeDtypeStruct((8, scenes), f32),
            jax.ShapeDtypeStruct((8, scenes), f32),
        ),
        in_specs=[vmem] * 4,
        out_specs=(vmem,) * 3,
        scratch_shapes=[
            pltpu.VMEM((turns, ncol, 8, scenes), f32),
            pltpu.VMEM((turns, nrow, 8, scenes), f32),
            dma((devices,)),
            dma((devices,)),
            dma((turns, ncol)),
            dma((turns, ncol)),
            dma((turns, nrow)),
            dma((turns, nrow)),
        ],
        compiler_params=pltpu.CompilerParams(
            collective_id=0, has_side_effects=True, vmem_limit_bytes=VMEM_LIMIT
        ),
        name="iterate",
    )(mat, diag, grad, panel)

    return pl.pallas_call(
        place_kernel,
        out_shape=(
            jax.ShapeDtypeStruct((6, 6, tile_rows, width), jnp.bfloat16),
            jax.ShapeDtypeStruct((6, tile_rows), f32),
            jax.ShapeDtypeStruct((6, tile_rows), f32),
        ),
        in_specs=[vmem] * 5,
        out_specs=(vmem,) * 3,
        compiler_params=pltpu.CompilerParams(vmem_limit_bytes=VMEM_LIMIT),
        name="place",
    )(recv.reshape(devices * rows, 6 * width), place, map_row, sol, res)


def solution(mesh):
    return jax.shard_map(
        shards,
        mesh=mesh,
        in_specs=(
            P(None, None, None, ("row", "col"), None),
            P(None, None, None, ("row", "col"), None),
            P(None, None, ("row", "col"), None),
            P(("row", "col"), None),
            P(("row", "col")),
            P(),
        ),
        out_specs=(P(None, None, "row", "col"), P(None, "row"), P(None, "row")),
        check_vma=False,
    )
```

```python
import functools

import jax
import jax.numpy as jnp
from jax import lax
from jax.experimental import pallas as pl
from jax.experimental.pallas import tpu as pltpu
from jax.sharding import PartitionSpec as P

ITERS = 3
CAMERA_DAMPING = 1.0
POINT_DAMPING = 1.0
LANES = 128
OTHER_ROWS = 64
OWN_ROWS = 32
ROWS = OTHER_ROWS + OWN_ROWS
PAIRS = [(x, y) for x in range(6) for y in range(x, 6)]
SPARE = [y * 8 + 6 + h for y in range(6) for h in range(2)] + list(range(48, 63))
NT = (((1,), (1,)), ((), ()))
MESH = pl.DeviceIdType.MESH
VMEM_LIMIT = 60 * 1024 * 1024


def total_of(terms):
    result = terms[0]
    for term in terms[1:]:
        result = result + term
    return result


def point_rows(cam, pt, err):
    hess = {}
    for i in range(3):
        for j in range(i, 3):
            value = total_of([pt[s][r][i] * pt[s][r][j] for s in range(2) for r in range(2)])
            hess[i, j] = value + POINT_DAMPING if i == j else value
    a, b, c = hess[0, 0], hess[0, 1], hess[0, 2]
    d, e, f = hess[1, 1], hess[1, 2], hess[2, 2]
    cof = {
        (0, 0): d * f - e * e,
        (0, 1): e * c - b * f,
        (0, 2): b * e - d * c,
        (1, 1): f * a - c * c,
        (1, 2): c * b - a * e,
        (2, 2): a * d - b * b,
    }
    scale = 1.0 / (a * cof[0, 0] + b * cof[0, 1] + c * cof[0, 2])
    inv = {key: value * scale for key, value in cof.items()}
    rhs = [-total_of([pt[s][r][i] * err[s][r] for s in range(2) for r in range(2)]) for i in range(3)]
    w = [
        [[total_of([cam[s][r][x] * pt[s][r][i] for r in range(2)]) for i in range(3)] for x in range(6)]
        for s in range(2)
    ]
    wv = [
        [
            [total_of([w[s][x][i] * inv[min(i, j), max(i, j)] for i in range(3)]) for j in range(3)]
            for x in range(6)
        ]
        for s in range(2)
    ]
    link = {
        (x, y): -total_of([wv[0][x][j] * w[1][y][j] for j in range(3)])
        for x in range(6)
        for y in range(6)
    }
    sides = []
    for s in range(2):
        rows = [
            total_of([cam[s][r][x] * cam[s][r][y] for r in range(2)])
            - total_of([wv[s][x][j] * w[s][y][j] for j in range(3)])
            for x, y in PAIRS
        ]
        rows += [
            -total_of([cam[s][r][x] * err[s][r] for r in range(2)])
            - total_of([wv[s][x][j] * rhs[j] for j in range(3)])
            for x in range(6)
        ]
        sides.append(rows)
    return link, sides[0], sides[1]


def assemble_kernel(
    nrow, ncol, cam_ref, pt_ref, err_ref, partner_ref, count_ref, map_ref,
    mat_ref, diag_ref, grad_ref, panel_ref, vals, acc,
):
    scn, points = partner_ref.shape
    scenes = map_ref.shape[1]
    blocks = points // LANES
    base = (lax.axis_index("row") * ncol + lax.axis_index("col")) * scn

    def point_block(jb, carry):
        lanes = pl.ds(pl.multiple_of(jb * LANES, LANES), LANES)
        take = lambda ref, *at: ref[at + (slice(None), lanes)].astype(jnp.float32)
        cam = [[[take(cam_ref, s, r, x) for x in range(6)] for r in range(2)] for s in range(2)]
        pt = [[[take(pt_ref, s, r, x) for x in range(3)] for r in range(2)] for s in range(2)]
        err = [[take(err_ref, s, r) for r in range(2)] for s in range(2)]
        link, own, other = point_rows(cam, pt, err)

        def put(row, value):
            vals[pl.ds(jb * (scn * ROWS) + row, scn, stride=ROWS), :] = value

        zero = jnp.zeros((scn, LANES), jnp.float32)
        for (x, y), value in link.items():
            put(y * 8 + x, value)
        for u in range(27):
            put(SPARE[u], other[u])
            put(OTHER_ROWS + u, own[u])
        put(OTHER_ROWS - 1, zero)
        for u in range(27, OWN_ROWS):
            put(OTHER_ROWS + u, zero)
        return carry

    lax.fori_loop(0, blocks, point_block, 0)
    acc[...] = jnp.zeros_like(acc)
    chunk = 256
    low = lax.broadcasted_iota(jnp.int32, (8, chunk), 0) < 6

    spot = lax.broadcasted_iota(jnp.int32, (chunk, points), 0).astype(jnp.float32).astype(jnp.bfloat16)
    one, nought = jnp.bfloat16(1), jnp.bfloat16(0)
    slot = lax.broadcasted_iota(jnp.int32, (OWN_ROWS, LANES), 1)

    def scene(s, own_sum):
        start = lambda jb: pl.multiple_of((jb * scn + s) * ROWS, 8)
        full = jnp.concatenate([vals[pl.ds(start(jb), OTHER_ROWS), :] for jb in range(blocks)], axis=1)
        high = full.astype(jnp.bfloat16)
        rest = (full - high.astype(jnp.float32)).astype(jnp.bfloat16)
        both = jnp.concatenate([high, rest], axis=0)
        live = count_ref[s]
        ids = partner_ref[pl.ds(s, 1), :]
        ids = jnp.where(lax.broadcasted_iota(jnp.int32, (1, points), 1) < live, ids, -1)
        for b in range(scenes // chunk):
            near = (ids - b * chunk).astype(jnp.float32).astype(jnp.bfloat16)
            onehot = jnp.where(spot == near, one, nought)
            sums = lax.dot_general(both, onehot, NT, preferred_element_type=jnp.float32)
            sums = sums[:OTHER_ROWS] + sums[OTHER_ROWS:]
            cols = slice(b * chunk, (b + 1) * chunk)
            acc[:, cols] += sums
            for y in range(6):
                part = jnp.where(low, sums[y * 8 : y * 8 + 8], 0.0)
                mat_ref[pl.ds(pl.multiple_of(s * 8, 8), 8), y * scenes + b * chunk : y * scenes + (b + 1) * chunk] = (
                    part.astype(jnp.bfloat16).astype(jnp.float32)
                )
        own = total_of(
            [
                jnp.where(slot < live - jb * LANES, vals[pl.ds(start(jb) + OTHER_ROWS, OWN_ROWS), :], 0.0)
                for jb in range(blocks)
            ]
        )
        own = jnp.sum(own, axis=1, keepdims=True)
        here = lax.broadcasted_iota(jnp.int32, (OWN_ROWS, scenes), 1) == base + s
        return own_sum + jnp.where(here, own, 0.0)

    own_sum = lax.fori_loop(0, scn, scene, jnp.zeros((OWN_ROWS, scenes), jnp.float32))
    diag_ref[...] = jnp.zeros_like(diag_ref)
    grad_ref[...] = jnp.zeros_like(grad_ref)
    for u in range(27):
        row = acc[SPARE[u] : SPARE[u] + 1, :] + own_sum[u : u + 1, :]
        if u < 21:
            x, y = PAIRS[u]
            diag_ref[y * 8 + x : y * 8 + x + 1, :] = row
            if x != y:
                diag_ref[x * 8 + y : x * 8 + y + 1, :] = row
        else:
            grad_ref[u - 21 : u - 20, :] = row

    rows = panel_ref.shape[1]
    group = scn // nrow
    line = lax.broadcasted_iota(jnp.int32, (scn * 8, scenes), 0)
    lane = lax.broadcasted_iota(jnp.int32, (scn * 8, scenes), 1) - base
    tiles = map_ref[...]
    mine = jnp.sum(jnp.where(lane == line // 8, tiles, 0), axis=1, keepdims=True)
    lower = (lane >= 0) & (lane < scn) & (tiles < mine)
    rank = jnp.sum(jnp.where(lower, 1, 0), axis=1, keepdims=True)
    param = line[:, :1] % 8
    target = (rank // group) * rows + param * group + rank % group
    target = jnp.where(param < 6, target, -1)
    order = jnp.where(
        lax.broadcasted_iota(jnp.int32, (scn * 8, nrow * rows), 1) == target, 1.0, 0.0
    ).T.astype(jnp.bfloat16)
    spots = jnp.where(
        lax.broadcasted_iota(jnp.int32, (scenes, scenes), 0) == map_ref[...], 1.0, 0.0
    ).astype(jnp.bfloat16)
    width = scenes // ncol
    ordered = []
    for y in range(6):
        piece = mat_ref[:, y * scenes : (y + 1) * scenes].astype(jnp.bfloat16)
        piece = jnp.dot(order, piece, preferred_element_type=jnp.float32).astype(jnp.bfloat16)
        ordered.append(lax.dot_general(piece, spots, NT, preferred_element_type=jnp.float32))
    for c in range(ncol):
        wide = jnp.concatenate([o[:, c * width : (c + 1) * width] for o in ordered], axis=1)
        for r in range(nrow):
            panel_ref[r * ncol + c] = wide[r * rows : (r + 1) * rows].astype(jnp.bfloat16)


def iterate_kernel(
    nrow, ncol, scn, mat_ref, diag_ref, grad_ref, panel_ref, recv_ref, sol_ref, res_ref,
    buf_col, buf_row, send_p, recv_p, send_c, recv_c, send_r, recv_r,
):
    row, col = lax.axis_index("row"), lax.axis_index("col")
    count = nrow * ncol
    me = row * ncol + col
    base = me * scn
    scenes = grad_ref.shape[1]

    barrier = pltpu.get_barrier_semaphore()

    def greet(off, carry):
        peer = lax.rem(me + off, count)
        pl.semaphore_signal(barrier, inc=1, device_id=(peer // ncol, lax.rem(peer, ncol)), device_id_type=MESH)
        return carry

    lax.fori_loop(1, count, greet, 0)
    pl.semaphore_wait(barrier, count - 1)

    def panel_copy(off):
        peer = lax.rem(me + off, count)
        return pltpu.make_async_remote_copy(
            src_ref=panel_ref.at[peer],
            dst_ref=recv_ref.at[me],
            send_sem=send_p.at[off],
            recv_sem=recv_p.at[off],
            device_id=(peer // ncol, lax.rem(peer, ncol)),
            device_id_type=MESH,
        )

    def gathered(value, buf, spot, turn, size, send, recv, device_of):
        buf[turn, spot] = value
        copies = []
        for off in range(1, size):
            copy = pltpu.make_async_remote_copy(
                src_ref=buf.at[turn, spot],
                dst_ref=buf.at[turn, spot],
                send_sem=send.at[turn, off],
                recv_sem=recv.at[turn, off],
                device_id=device_of(lax.rem(spot + off, size)),
                device_id_type=MESH,
            )
            copy.start()
            copies.append(copy)
        for copy in copies:
            copy.wait()
        return total_of([buf[turn, i] for i in range(size)])

    def all_sum(value, turn):
        value = gathered(value, buf_col, col, turn, ncol, send_c, recv_c, lambda p: (row, p))
        return gathered(value, buf_row, row, turn, nrow, send_r, recv_r, lambda p: (p, col))

    def start_panels(turn):
        def step(off, carry):
            panel_copy(off).start()
            return carry

        lax.fori_loop(1 + turn * (count - 1) // ITERS, 1 + (turn + 1) * (count - 1) // ITERS, step, 0)

    lane = lax.broadcasted_iota(jnp.int32, (8, scenes), 1)

    def local_product(vector):
        flat = jnp.concatenate([vector[y : y + 1] for y in range(6)], axis=1)

        out = jnp.zeros((8, scenes), jnp.float32)
        owns, folds = [], []
        for s in range(scn):
            owns.append(jnp.sum(jnp.where(lane == base + s, vector, 0.0), axis=1, keepdims=True))
        back = None
        for s in range(scn):
            part = mat_ref[s * 8 : s * 8 + 8, :]
            folds.append(jnp.sum(part * flat, axis=1, keepdims=True))
            back = part * owns[s] if back is None else back + part * owns[s]
        for s in range(scn):
            out = out + jnp.where(lane == base + s, folds[s], 0.0)
        back = jnp.sum(back, axis=0, keepdims=True)
        for y in range(6):
            out = out + diag_ref[y * 8 : y * 8 + 8, :] * vector[y : y + 1]
        back = jnp.concatenate(
            [back[:, y * scenes : (y + 1) * scenes] for y in range(6)]
            + [jnp.zeros((2, scenes), jnp.float32)],
            axis=0,
        )
        return out + back

    def inner(first, second):
        return jnp.sum(jnp.sum(first * second, axis=1, keepdims=True), axis=0, keepdims=True)

    remainder = all_sum(grad_ref[...], 0)
    recv_ref[me] = panel_ref[me]
    result = jnp.zeros_like(remainder)
    direction = remainder
    norm_now = inner(remainder, remainder)
    for turn in range(ITERS):
        start_panels(turn)
        image = CAMERA_DAMPING * direction + all_sum(local_product(direction), turn + 1)
        size = norm_now / inner(direction, image)
        result = result + size * direction
        remainder = remainder - size * image
        norm_next = inner(remainder, remainder)
        direction = remainder + norm_next / norm_now * direction
        norm_now = norm_next
    sol_ref[...] = result
    res_ref[...] = remainder

    def finish(off, carry):
        panel_copy(off).wait()
        return carry

    lax.fori_loop(1, count, finish, 0)


def place_kernel(rows, scn, recv_ref, map_ref, sol_ref, res_ref, coupling_ref, update_ref, residual_ref):
    width, tile_rows = coupling_ref.shape[2:]
    held = recv_ref.shape[0]
    scenes = map_ref.shape[1]
    group = scn * tile_rows // scenes
    first = lax.axis_index("row") * tile_rows
    tiles = map_ref[...]
    place = lax.broadcasted_iota(jnp.int32, (tile_rows, scenes), 0) + first
    lane = lax.broadcasted_iota(jnp.int32, (tile_rows, scenes), 1)
    source = jnp.sum(jnp.where(tiles == place, lane // scn, 0), axis=1, keepdims=True)
    lower = (lane // scn == source) & (tiles >= first) & (tiles < place)
    spot = source * rows + jnp.sum(jnp.where(lower, 1, 0), axis=1, keepdims=True)
    flipped = recv_ref[...].T
    for x in range(6):
        index = lax.broadcasted_iota(jnp.int32, (tile_rows, held), 1) - x * group
        chosen = jnp.where(index == spot, 1.0, 0.0).astype(jnp.bfloat16)
        block = lax.dot_general(flipped, chosen, NT, preferred_element_type=jnp.float32)
        coupling_ref[x] = block.astype(jnp.bfloat16).reshape(6, width, tile_rows)
    chosen = jnp.where(tiles == place, 1.0, 0.0).astype(jnp.bfloat16)
    for source, target in ((sol_ref, update_ref), (res_ref, residual_ref)):
        left = source[...]
        moved = None
        for unused in range(3):
            short = left.astype(jnp.bfloat16)
            left = left - short.astype(jnp.float32)
            part = lax.dot_general(short, chosen, NT, preferred_element_type=jnp.float32)
            moved = part if moved is None else moved + part
        target[...] = moved[:6]


def shards(cam_jac, pt_jac, resid, partner, count, tile_map):
    nrow = lax.axis_size("row")
    ncol = lax.axis_size("col")
    scenes = tile_map.shape[0]
    scn, points = partner.shape
    devices = nrow * ncol
    tile_rows = scenes // nrow
    width = scenes // ncol
    group = scn // nrow
    rows = -(-6 * group // 8) * 8
    map_row = tile_map.reshape(1, scenes)

    vmem = pl.BlockSpec(memory_space=pltpu.VMEM)
    f32 = jnp.float32
    mat, diag, grad, panel = pl.pallas_call(
        functools.partial(assemble_kernel, nrow, ncol),
        out_shape=(
            jax.ShapeDtypeStruct((scn * 8, 6 * scenes), f32),
            jax.ShapeDtypeStruct((48, scenes), f32),
            jax.ShapeDtypeStruct((8, scenes), f32),
            jax.ShapeDtypeStruct((devices, rows, 6 * width), jnp.bfloat16),
        ),
        in_specs=[vmem] * 4 + [pl.BlockSpec(memory_space=pltpu.SMEM), vmem],
        out_specs=(vmem,) * 4,
        scratch_shapes=[
            pltpu.VMEM((points // LANES * scn * ROWS, LANES), f32),
            pltpu.VMEM((OTHER_ROWS, scenes), f32),
        ],
        compiler_params=pltpu.CompilerParams(vmem_limit_bytes=VMEM_LIMIT),
        name="assemble",
    )(cam_jac, pt_jac, resid, partner, count, map_row)

    turns = ITERS + 1
    dma = pltpu.SemaphoreType.DMA
    recv, sol, res = pl.pallas_call(
        functools.partial(iterate_kernel, nrow, ncol, scn),
        out_shape=(
            jax.ShapeDtypeStruct((devices, rows, 6 * width), jnp.bfloat16),
            jax.ShapeDtypeStruct((8, scenes), f32),
            jax.ShapeDtypeStruct((8, scenes), f32),
        ),
        in_specs=[vmem] * 4,
        out_specs=(vmem,) * 3,
        scratch_shapes=[
            pltpu.VMEM((turns, ncol, 8, scenes), f32),
            pltpu.VMEM((turns, nrow, 8, scenes), f32),
            dma((devices,)),
            dma((devices,)),
            dma((turns, ncol)),
            dma((turns, ncol)),
            dma((turns, nrow)),
            dma((turns, nrow)),
        ],
        compiler_params=pltpu.CompilerParams(
            collective_id=0, has_side_effects=True, vmem_limit_bytes=VMEM_LIMIT
        ),
        name="iterate",
    )(mat, diag, grad, panel)

    coupling, update, residual = pl.pallas_call(
        functools.partial(place_kernel, rows, scn),
        out_shape=(
            jax.ShapeDtypeStruct((6, 6, width, tile_rows), jnp.bfloat16),
            jax.ShapeDtypeStruct((6, tile_rows), f32),
            jax.ShapeDtypeStruct((6, tile_rows), f32),
        ),
        in_specs=[vmem] * 4,
        out_specs=(vmem,) * 3,
        compiler_params=pltpu.CompilerParams(vmem_limit_bytes=VMEM_LIMIT),
        name="place",
    )(recv.reshape(devices * rows, 6 * width), map_row, sol, res)
    return jnp.swapaxes(coupling, 2, 3), update, residual


def solution(mesh):
    return jax.shard_map(
        shards,
        mesh=mesh,
        in_specs=(
            P(None, None, None, ("row", "col"), None),
            P(None, None, None, ("row", "col"), None),
            P(None, None, ("row", "col"), None),
            P(("row", "col"), None),
            P(("row", "col")),
            P(),
        ),
        out_specs=(P(None, None, "row", "col"), P(None, "row"), P(None, "row")),
        check_vma=False,
    )
```

```python
import functools

import jax
import jax.numpy as jnp
from jax import lax
from jax.experimental import pallas as pl
from jax.experimental.pallas import tpu as pltpu
from jax.sharding import PartitionSpec as P

ITERS = 3
CAMERA_DAMPING = 1.0
POINT_DAMPING = 1.0
LANES = 128
OTHER_ROWS = 64
OWN_ROWS = 32
ROWS = OTHER_ROWS + OWN_ROWS
PAIRS = [(x, y) for x in range(6) for y in range(x, 6)]
SPARE = [y * 8 + 6 + h for y in range(6) for h in range(2)] + list(range(48, 63))
NT = (((1,), (1,)), ((), ()))
MESH = pl.DeviceIdType.MESH
VMEM_LIMIT = 60 * 1024 * 1024


def total_of(terms):
    result = terms[0]
    for term in terms[1:]:
        result = result + term
    return result


def point_rows(cam, pt, err):
    hess = {}
    for i in range(3):
        for j in range(i, 3):
            value = total_of([pt[s][r][i] * pt[s][r][j] for s in range(2) for r in range(2)])
            hess[i, j] = value + POINT_DAMPING if i == j else value
    a, b, c = hess[0, 0], hess[0, 1], hess[0, 2]
    d, e, f = hess[1, 1], hess[1, 2], hess[2, 2]
    cof = {
        (0, 0): d * f - e * e,
        (0, 1): e * c - b * f,
        (0, 2): b * e - d * c,
        (1, 1): f * a - c * c,
        (1, 2): c * b - a * e,
        (2, 2): a * d - b * b,
    }
    scale = 1.0 / (a * cof[0, 0] + b * cof[0, 1] + c * cof[0, 2])
    inv = {key: value * scale for key, value in cof.items()}
    rhs = [-total_of([pt[s][r][i] * err[s][r] for s in range(2) for r in range(2)]) for i in range(3)]
    w = [
        [[total_of([cam[s][r][x] * pt[s][r][i] for r in range(2)]) for i in range(3)] for x in range(6)]
        for s in range(2)
    ]
    wv = [
        [
            [total_of([w[s][x][i] * inv[min(i, j), max(i, j)] for i in range(3)]) for j in range(3)]
            for x in range(6)
        ]
        for s in range(2)
    ]
    link = {
        (x, y): -total_of([wv[0][x][j] * w[1][y][j] for j in range(3)])
        for x in range(6)
        for y in range(6)
    }
    sides = []
    for s in range(2):
        rows = [
            total_of([cam[s][r][x] * cam[s][r][y] for r in range(2)])
            - total_of([wv[s][x][j] * w[s][y][j] for j in range(3)])
            for x, y in PAIRS
        ]
        rows += [
            -total_of([cam[s][r][x] * err[s][r] for r in range(2)])
            - total_of([wv[s][x][j] * rhs[j] for j in range(3)])
            for x in range(6)
        ]
        sides.append(rows)
    return link, sides[0], sides[1]


def assemble_kernel(
    nrow, ncol, cam_ref, pt_ref, err_ref, partner_ref, count_ref, map_ref,
    mat_ref, diag_ref, grad_ref, panel_ref, vals, acc,
):
    scn, points = partner_ref.shape
    scenes = map_ref.shape[1]
    blocks = points // LANES
    base = (lax.axis_index("row") * ncol + lax.axis_index("col")) * scn

    def point_block(jb, carry):
        lanes = pl.ds(pl.multiple_of(jb * LANES, LANES), LANES)
        take = lambda ref, *at: ref[at + (slice(None), lanes)].astype(jnp.float32)
        cam = [[[take(cam_ref, s, r, x) for x in range(6)] for r in range(2)] for s in range(2)]
        pt = [[[take(pt_ref, s, r, x) for x in range(3)] for r in range(2)] for s in range(2)]
        err = [[take(err_ref, s, r) for r in range(2)] for s in range(2)]
        link, own, other = point_rows(cam, pt, err)

        def put(row, value):
            vals[pl.ds(jb * (scn * ROWS) + row, scn, stride=ROWS), :] = value

        zero = jnp.zeros((scn, LANES), jnp.float32)
        for (x, y), value in link.items():
            put(y * 8 + x, value)
        for u in range(27):
            put(SPARE[u], other[u])
            put(OTHER_ROWS + u, own[u])
        put(OTHER_ROWS - 1, zero)
        for u in range(27, OWN_ROWS):
            put(OTHER_ROWS + u, zero)
        return carry

    lax.fori_loop(0, blocks, point_block, 0)
    acc[...] = jnp.zeros_like(acc)
    chunk = 256
    low = lax.broadcasted_iota(jnp.int32, (8, chunk), 0) < 6

    spot = lax.broadcasted_iota(jnp.int32, (chunk, points), 0).astype(jnp.float32).astype(jnp.bfloat16)
    one, nought = jnp.bfloat16(1), jnp.bfloat16(0)
    slot = lax.broadcasted_iota(jnp.int32, (OWN_ROWS, LANES), 1)

    def scene(s, own_sum):
        start = lambda jb: pl.multiple_of((jb * scn + s) * ROWS, 8)
        full = jnp.concatenate([vals[pl.ds(start(jb), OTHER_ROWS), :] for jb in range(blocks)], axis=1)
        high = full.astype(jnp.bfloat16)
        rest = (full - high.astype(jnp.float32)).astype(jnp.bfloat16)
        both = jnp.concatenate([high, rest], axis=0)
        live = count_ref[s]
        ids = partner_ref[pl.ds(s, 1), :]
        ids = jnp.where(lax.broadcasted_iota(jnp.int32, (1, points), 1) < live, ids, -1)
        for b in range(scenes // chunk):
            near = (ids - b * chunk).astype(jnp.float32).astype(jnp.bfloat16)
            onehot = jnp.where(spot == near, one, nought)
            sums = lax.dot_general(both, onehot, NT, preferred_element_type=jnp.float32)
            sums = sums[:OTHER_ROWS] + sums[OTHER_ROWS:]
            cols = slice(b * chunk, (b + 1) * chunk)
            acc[:, cols] += sums
            for y in range(6):
                part = jnp.where(low, sums[y * 8 : y * 8 + 8], 0.0)
                mat_ref[pl.ds(pl.multiple_of(s * 8, 8), 8), y * scenes + b * chunk : y * scenes + (b + 1) * chunk] = (
                    part.astype(jnp.bfloat16).astype(jnp.float32)
                )
        own = total_of(
            [
                jnp.where(slot < live - jb * LANES, vals[pl.ds(start(jb) + OTHER_ROWS, OWN_ROWS), :], 0.0)
                for jb in range(blocks)
            ]
        )
        own = jnp.sum(own, axis=1, keepdims=True)
        here = lax.broadcasted_iota(jnp.int32, (OWN_ROWS, scenes), 1) == base + s
        return own_sum + jnp.where(here, own, 0.0)

    own_sum = lax.fori_loop(0, scn, scene, jnp.zeros((OWN_ROWS, scenes), jnp.float32), unroll=4)
    diag_ref[...] = jnp.zeros_like(diag_ref)
    grad_ref[...] = jnp.zeros_like(grad_ref)
    for u in range(27):
        row = acc[SPARE[u] : SPARE[u] + 1, :] + own_sum[u : u + 1, :]
        if u < 21:
            x, y = PAIRS[u]
            diag_ref[y * 8 + x : y * 8 + x + 1, :] = row
            if x != y:
                diag_ref[x * 8 + y : x * 8 + y + 1, :] = row
        else:
            grad_ref[u - 21 : u - 20, :] = row

    rows = panel_ref.shape[1]
    group = scn // nrow
    line = lax.broadcasted_iota(jnp.int32, (scn * 8, scenes), 0)
    lane = lax.broadcasted_iota(jnp.int32, (scn * 8, scenes), 1) - base
    tiles = map_ref[...]
    mine = jnp.sum(jnp.where(lane == line // 8, tiles, 0), axis=1, keepdims=True)
    lower = (lane >= 0) & (lane < scn) & (tiles < mine)
    rank = jnp.sum(jnp.where(lower, 1, 0), axis=1, keepdims=True)
    param = line[:, :1] % 8
    target = (rank // group) * rows + param * group + rank % group
    target = jnp.where(param < 6, target, -1)
    order = jnp.where(
        lax.broadcasted_iota(jnp.int32, (scn * 8, nrow * rows), 1) == target, 1.0, 0.0
    ).T.astype(jnp.bfloat16)
    spots = jnp.where(
        lax.broadcasted_iota(jnp.int32, (scenes, scenes), 0) == map_ref[...], 1.0, 0.0
    ).astype(jnp.bfloat16)
    width = scenes // ncol
    ordered = []
    for y in range(6):
        piece = mat_ref[:, y * scenes : (y + 1) * scenes].astype(jnp.bfloat16)
        piece = jnp.dot(order, piece, preferred_element_type=jnp.float32).astype(jnp.bfloat16)
        ordered.append(lax.dot_general(piece, spots, NT, preferred_element_type=jnp.float32))
    for c in range(ncol):
        wide = jnp.concatenate([o[:, c * width : (c + 1) * width] for o in ordered], axis=1)
        for r in range(nrow):
            panel_ref[r * ncol + c] = wide[r * rows : (r + 1) * rows].astype(jnp.bfloat16)


def iterate_kernel(
    nrow, ncol, scn, mat_ref, diag_ref, grad_ref, panel_ref, recv_ref, sol_ref, res_ref,
    buf_col, buf_row, send_p, recv_p, send_c, recv_c, send_r, recv_r,
):
    row, col = lax.axis_index("row"), lax.axis_index("col")
    count = nrow * ncol
    me = row * ncol + col
    base = me * scn
    scenes = grad_ref.shape[1]

    barrier = pltpu.get_barrier_semaphore()

    def greet(off, carry):
        peer = lax.rem(me + off, count)
        pl.semaphore_signal(barrier, inc=1, device_id=(peer // ncol, lax.rem(peer, ncol)), device_id_type=MESH)
        return carry

    lax.fori_loop(1, count, greet, 0)
    pl.semaphore_wait(barrier, count - 1)

    def panel_copy(off):
        peer = lax.rem(me + off, count)
        return pltpu.make_async_remote_copy(
            src_ref=panel_ref.at[peer],
            dst_ref=recv_ref.at[me],
            send_sem=send_p.at[off],
            recv_sem=recv_p.at[off],
            device_id=(peer // ncol, lax.rem(peer, ncol)),
            device_id_type=MESH,
        )

    def gathered(value, buf, spot, turn, size, send, recv, device_of, stage):
        buf[turn, spot] = value
        copies = []
        for off in range(1, size):
            copy = pltpu.make_async_remote_copy(
                src_ref=buf.at[turn, spot],
                dst_ref=buf.at[turn, spot],
                send_sem=send.at[turn, off],
                recv_sem=recv.at[turn, off],
                device_id=device_of(lax.rem(spot + off, size)),
                device_id_type=MESH,
            )
            copy.start()
            copies.append(copy)
        start_panels(stage)
        for copy in copies:
            copy.wait()
        return total_of([buf[turn, i] for i in range(size)])

    def all_sum(value, turn):
        value = gathered(value, buf_col, col, turn, ncol, send_c, recv_c, lambda p: (row, p), 2 * turn)
        return gathered(value, buf_row, row, turn, nrow, send_r, recv_r, lambda p: (p, col), 2 * turn + 1)

    stages = 2 * (ITERS + 1)

    def start_panels(turn):
        def step(off, carry):
            panel_copy(off).start()
            return carry

        lax.fori_loop(1 + turn * (count - 1) // stages, 1 + (turn + 1) * (count - 1) // stages, step, 0)

    lane = lax.broadcasted_iota(jnp.int32, (8, scenes), 1)

    def local_product(vector):
        flat = jnp.concatenate([vector[y : y + 1] for y in range(6)], axis=1)

        out = jnp.zeros((8, scenes), jnp.float32)
        owns, folds = [], []
        for s in range(scn):
            owns.append(jnp.sum(jnp.where(lane == base + s, vector, 0.0), axis=1, keepdims=True))
        back = None
        for s in range(scn):
            part = mat_ref[s * 8 : s * 8 + 8, :]
            folds.append(jnp.sum(part * flat, axis=1, keepdims=True))
            back = part * owns[s] if back is None else back + part * owns[s]
        for s in range(scn):
            out = out + jnp.where(lane == base + s, folds[s], 0.0)
        back = jnp.sum(back, axis=0, keepdims=True)
        for y in range(6):
            out = out + diag_ref[y * 8 : y * 8 + 8, :] * vector[y : y + 1]
        back = jnp.concatenate(
            [back[:, y * scenes : (y + 1) * scenes] for y in range(6)]
            + [jnp.zeros((2, scenes), jnp.float32)],
            axis=0,
        )
        return out + back

    def inner(first, second):
        return jnp.sum(jnp.sum(first * second, axis=1, keepdims=True), axis=0, keepdims=True)

    remainder = all_sum(grad_ref[...], 0)
    recv_ref[me] = panel_ref[me]
    result = jnp.zeros_like(remainder)
    direction = remainder
    norm_now = inner(remainder, remainder)
    for turn in range(ITERS):
        image = CAMERA_DAMPING * direction + all_sum(local_product(direction), turn + 1)
        size = norm_now / inner(direction, image)
        result = result + size * direction
        remainder = remainder - size * image
        norm_next = inner(remainder, remainder)
        direction = remainder + norm_next / norm_now * direction
        norm_now = norm_next
    sol_ref[...] = result
    res_ref[...] = remainder

    def finish(off, carry):
        panel_copy(off).wait()
        return carry

    lax.fori_loop(1, count, finish, 0)


def place_kernel(rows, scn, recv_ref, map_ref, sol_ref, res_ref, coupling_ref, update_ref, residual_ref):
    width, tile_rows = coupling_ref.shape[2:]
    held = recv_ref.shape[0]
    scenes = map_ref.shape[1]
    group = scn * tile_rows // scenes
    first = lax.axis_index("row") * tile_rows
    tiles = map_ref[...]
    place = lax.broadcasted_iota(jnp.int32, (tile_rows, scenes), 0) + first
    lane = lax.broadcasted_iota(jnp.int32, (tile_rows, scenes), 1)
    source = jnp.sum(jnp.where(tiles == place, lane // scn, 0), axis=1, keepdims=True)
    lower = (lane // scn == source) & (tiles >= first) & (tiles < place)
    spot = source * rows + jnp.sum(jnp.where(lower, 1, 0), axis=1, keepdims=True)
    flipped = recv_ref[...].T
    for x in range(6):
        index = lax.broadcasted_iota(jnp.int32, (tile_rows, held), 1) - x * group
        chosen = jnp.where(index == spot, 1.0, 0.0).astype(jnp.bfloat16)
        block = lax.dot_general(flipped, chosen, NT, preferred_element_type=jnp.float32)
        coupling_ref[x] = block.astype(jnp.bfloat16).reshape(6, width, tile_rows)
    chosen = jnp.where(tiles == place, 1.0, 0.0).astype(jnp.bfloat16)
    for source, target in ((sol_ref, update_ref), (res_ref, residual_ref)):
        left = source[...]
        moved = None
        for unused in range(3):
            short = left.astype(jnp.bfloat16)
            left = left - short.astype(jnp.float32)
            part = lax.dot_general(short, chosen, NT, preferred_element_type=jnp.float32)
            moved = part if moved is None else moved + part
        target[...] = moved[:6]


def shards(cam_jac, pt_jac, resid, partner, count, tile_map):
    nrow = lax.axis_size("row")
    ncol = lax.axis_size("col")
    scenes = tile_map.shape[0]
    scn, points = partner.shape
    devices = nrow * ncol
    tile_rows = scenes // nrow
    width = scenes // ncol
    group = scn // nrow
    rows = -(-6 * group // 8) * 8
    map_row = tile_map.reshape(1, scenes)

    vmem = pl.BlockSpec(memory_space=pltpu.VMEM)
    f32 = jnp.float32
    mat, diag, grad, panel = pl.pallas_call(
        functools.partial(assemble_kernel, nrow, ncol),
        out_shape=(
            jax.ShapeDtypeStruct((scn * 8, 6 * scenes), f32),
            jax.ShapeDtypeStruct((48, scenes), f32),
            jax.ShapeDtypeStruct((8, scenes), f32),
            jax.ShapeDtypeStruct((devices, rows, 6 * width), jnp.bfloat16),
        ),
        in_specs=[vmem] * 4 + [pl.BlockSpec(memory_space=pltpu.SMEM), vmem],
        out_specs=(vmem,) * 4,
        scratch_shapes=[
            pltpu.VMEM((points // LANES * scn * ROWS, LANES), f32),
            pltpu.VMEM((OTHER_ROWS, scenes), f32),
        ],
        compiler_params=pltpu.CompilerParams(vmem_limit_bytes=VMEM_LIMIT),
        name="assemble",
    )(cam_jac, pt_jac, resid, partner, count, map_row)

    turns = ITERS + 1
    dma = pltpu.SemaphoreType.DMA
    recv, sol, res = pl.pallas_call(
        functools.partial(iterate_kernel, nrow, ncol, scn),
        out_shape=(
            jax.ShapeDtypeStruct((devices, rows, 6 * width), jnp.bfloat16),
            jax.ShapeDtypeStruct((8, scenes), f32),
            jax.ShapeDtypeStruct((8, scenes), f32),
        ),
        in_specs=[vmem] * 4,
        out_specs=(vmem,) * 3,
        scratch_shapes=[
            pltpu.VMEM((turns, ncol, 8, scenes), f32),
            pltpu.VMEM((turns, nrow, 8, scenes), f32),
            dma((devices,)),
            dma((devices,)),
            dma((turns, ncol)),
            dma((turns, ncol)),
            dma((turns, nrow)),
            dma((turns, nrow)),
        ],
        compiler_params=pltpu.CompilerParams(
            collective_id=0, has_side_effects=True, vmem_limit_bytes=VMEM_LIMIT
        ),
        name="iterate",
    )(mat, diag, grad, panel)

    coupling, update, residual = pl.pallas_call(
        functools.partial(place_kernel, rows, scn),
        out_shape=(
            jax.ShapeDtypeStruct((6, 6, width, tile_rows), jnp.bfloat16),
            jax.ShapeDtypeStruct((6, tile_rows), f32),
            jax.ShapeDtypeStruct((6, tile_rows), f32),
        ),
        in_specs=[vmem] * 4,
        out_specs=(vmem,) * 3,
        compiler_params=pltpu.CompilerParams(vmem_limit_bytes=VMEM_LIMIT),
        name="place",
    )(recv.reshape(devices * rows, 6 * width), map_row, sol, res)
    return jnp.swapaxes(coupling, 2, 3), update, residual


def solution(mesh):
    return jax.shard_map(
        shards,
        mesh=mesh,
        in_specs=(
            P(None, None, None, ("row", "col"), None),
            P(None, None, None, ("row", "col"), None),
            P(None, None, ("row", "col"), None),
            P(("row", "col"), None),
            P(("row", "col")),
            P(),
        ),
        out_specs=(P(None, None, "row", "col"), P(None, "row"), P(None, "row")),
        check_vma=False,
    )
```
